1024 devices in a mesh: clus: 16 (over y, core), sub: 64 (over z, x).
Axes of the slice: x: 4, y: 8, z: 16, core: 2. Of those that a mesh axis runs over, the one named last changes fastest.
Arguments:
- dual_ops: bfloat16 [1024, 1024, 1024], P(('clus', 'sub')), as said below
- dual_rhs: bfloat16 [1024, 1024, 128], P(('clus', 'sub')), as said below
- partner: int32 [1024, 28], P(('clus', 'sub')), may hold values from -1 to 1791, as said below
- cluster_basis: bfloat16 [1024, 192, 896], P(('clus', 'sub')), as said below
- global_basis: bfloat16 [1024, 6, 896], P(('clus', 'sub')), as said below
- cluster_inverse: float32 [16, 192, 192], P('clus'), as said below
- global_inverse: float32 [96, 96], replicated, as said below
Outputs:
- multipliers: float32 [1024, 1024, 128], P(('clus', 'sub'))
The draws below stay inside these ranges and needn't reach their ends.
Inputs may be any that keep to these rules, and one draw needn't show every extreme that they name: partner[s, b] is -1 or a value g naming block g % 28 of subdomain (s // 64) * 64 + g // 28, another subdomain of the same cluster, whose entry for that block names block b of s back; two subdomains share at most 1 glued blocks, and some two share exactly 1. Each dual_ops[s] is symmetric positive definite. `dual_rhs`: the copies of a multiplier agree: on every row where weight is 1/2 the row equals the same row of the partner copy. `cluster_basis`: on every interface row glued to a partner block the modes equal those of the partner row. `global_basis`: on every interface row glued to a partner block the modes equal those of the partner row. Each cluster_inverse[c] is symmetric positive definite. global_inverse is symmetric positive definite.
All inputs are finite; a program needn't handle non-finite values.
Results may differ from the reference program's by a relative error of at most 0.001.
Values sent between devices are 32-bit elements; how exact they have to be, the bound alone decides.
No kernel may reach another device: no remote copies, remote signals or barrier semaphores. Data moves between devices by JAX's collectives and lax.ppermute only.
A program may use at most 32 MiB of HBM per device.

```python
import math
import jax
import jax.numpy as jnp
from jax import lax

NB = 1024
FACE = 64
BLK = 32
R = 128
KC = 192
MODES = 6
ITERS = 3
NIS = 896
NIB = 28
CLUSTERS = 16
CSUB = 64
SUBS = 1024
KG = 96


def link_table(key):
    base = jax.random.fold_in(key, 101)

    def one_cluster(cluster_key):
        key_label, key_order, key_keep = jax.random.split(cluster_key, 3)
        labels = jax.random.permutation(key_label, CSUB)
        block_order = jax.vmap(lambda inner_key: jax.random.permutation(inner_key, NIB))(jax.random.split(key_order, CSUB))
        places = jnp.arange(CSUB)[:, None]
        link_ids = jnp.arange(NIB)[None, :]
        residue = link_ids % CSUB
        mates = (residue - places) % CSUB
        lowest = jnp.minimum(places, mates)
        coins = jax.random.randint(key_keep, (CSUB, NIB), 0, 8)
        kept = (coins[lowest, jnp.broadcast_to(link_ids, (CSUB, NIB))] > 0) | (residue == 0)
        living = kept & (mates != places)
        mate_block = block_order[mates, jnp.broadcast_to(link_ids, (CSUB, NIB))]
        values = jnp.where(living, labels[mates] * NIB + mate_block, -1).astype(jnp.int32)
        target_rows = jnp.broadcast_to(labels[:, None], (CSUB, NIB))
        return jnp.zeros((CSUB, NIB), jnp.int32).at[target_rows, block_order].set(values)
    tables = jax.vmap(one_cluster)(jax.random.split(base, CLUSTERS))
    return tables.reshape(SUBS, NIB).astype(jnp.int32)


def agree_inner(values, partner_ids):
    columns = values.shape[2]
    blocks = values.reshape(CLUSTERS, CSUB * NIB, BLK, columns)
    own_ids = jnp.arange(CSUB * NIB)[None, :]
    flat_ids = partner_ids.reshape(CLUSTERS, CSUB * NIB)
    source = jnp.where((flat_ids >= 0) & (flat_ids < own_ids), flat_ids, own_ids).astype(jnp.int32)
    picked = jax.vmap(lambda block_set, index_set: jnp.take(block_set, index_set, axis=0))(blocks, source)
    return picked.reshape(SUBS, NIS, columns)


def agree_faces(values):
    lower_face = jnp.concatenate([values[:CSUB, :FACE], values[:SUBS - CSUB, FACE:2 * FACE]], axis=0)
    return jnp.concatenate([lower_face, values[:, FACE:]], axis=1)


def draw_partner(key, part):
    return link_table(key)


def draw_dual_ops(key, part):
    base = jax.random.fold_in(key, 303)

    def one_operator(inner_key):
        key_raw, key_diag = jax.random.split(inner_key)
        raw = jax.random.normal(key_raw, (NB, NB), jnp.float32)
        symmetric = (raw + raw.T) * (1.0 / math.sqrt(2.0 * NB))
        diagonal = jax.random.uniform(key_diag, (NB,), jnp.float32, 2.5, 6.0)
        return (jnp.diag(diagonal) + symmetric).astype(jnp.bfloat16)
    return lax.map(one_operator, jax.random.split(base, SUBS))


def draw_dual_rhs(key, part):
    partner_ids = link_table(key)
    noise_key = jax.random.fold_in(key, 202)
    values = jax.random.normal(noise_key, (SUBS, NB, R), jnp.float32)
    ramp = 1.0 + 2.0 * (jnp.arange(SUBS) % CSUB).astype(jnp.float32) / (CSUB - 1)
    values = values * ramp[:, None, None]
    values = agree_faces(values)
    interior = agree_inner(values[:, 2 * FACE:], partner_ids)
    values = jnp.concatenate([values[:, :2 * FACE], interior], axis=1)
    return values.astype(jnp.bfloat16)


def draw_cluster_basis(key, part):
    partner_ids = link_table(key)
    noise_key = jax.random.fold_in(key, 404)
    values = jax.random.normal(noise_key, (SUBS, NIS, KC), jnp.float32) * (1.0 / math.sqrt(NIS))
    values = agree_inner(values, partner_ids)
    return jnp.transpose(values, (0, 2, 1)).astype(jnp.bfloat16)


def draw_global_basis(key, part):
    partner_ids = link_table(key)
    noise_key = jax.random.fold_in(key, 505)
    values = jax.random.normal(noise_key, (SUBS, NIS, MODES), jnp.float32) * (1.0 / math.sqrt(NIS))
    values = agree_inner(values, partner_ids)
    return jnp.transpose(values, (0, 2, 1)).astype(jnp.bfloat16)


def definite_block(inner_key, order_size, scale):
    key_raw, key_diag = jax.random.split(inner_key)
    raw = jax.random.normal(key_raw, (order_size, order_size), jnp.float32)
    symmetric = (raw + raw.T) * (0.4 / math.sqrt(2.0 * order_size))
    diagonal = jax.random.uniform(key_diag, (order_size,), jnp.float32, 1.0, 2.0)
    return (jnp.diag(diagonal) + symmetric) * scale


def draw_cluster_inverse(key, part):
    base = jax.random.fold_in(key, 606)
    scale = 1.0 / math.sqrt(CSUB)
    return jax.vmap(lambda inner_key: definite_block(inner_key, KC, scale))(jax.random.split(base, CLUSTERS))


def draw_global_inverse(key, part):
    base = jax.random.fold_in(key, 707)
    return definite_block(base, KG, 1.0 / math.sqrt(CSUB))


def setup_inputs(seed: int = 0) -> dict:
    streams_of = jax.random.split(jax.random.key(seed), 8)
    dual_ops = draw_dual_ops(jax.random.fold_in(streams_of[7], 71), 0)
    dual_rhs = draw_dual_rhs(jax.random.fold_in(streams_of[7], 71), 0)
    partner = draw_partner(jax.random.fold_in(streams_of[7], 71), 0)
    cluster_basis = draw_cluster_basis(jax.random.fold_in(streams_of[7], 71), 0)
    global_basis = draw_global_basis(jax.random.fold_in(streams_of[7], 71), 0)
    cluster_inverse = draw_cluster_inverse(jax.random.fold_in(streams_of[7], 71), 0)
    global_inverse = draw_global_inverse(jax.random.fold_in(streams_of[7], 71), 0)
    return dict(dual_ops=dual_ops, dual_rhs=dual_rhs, partner=partner, cluster_basis=cluster_basis, global_basis=global_basis, cluster_inverse=cluster_inverse, global_inverse=global_inverse)


PRECISE = lax.Precision.HIGHEST


def partner_copy(values, partner):
    load_cases = values.shape[2]
    blocks = values[:, 2 * FACE:].reshape(CLUSTERS, CSUB * NIB, BLK, load_cases)
    partner_ids = partner.reshape(CLUSTERS, CSUB * NIB)
    linked = partner_ids >= 0
    safe_ids = jnp.where(linked, partner_ids, 0).astype(jnp.int32)
    picked = jax.vmap(lambda block_set, index_set: jnp.take(block_set, index_set, axis=0))(blocks, safe_ids)
    picked = jnp.where(linked[:, :, None, None], picked, jnp.zeros_like(picked))
    picked = picked.reshape(SUBS, NIB * BLK, load_cases)
    zero_rim = jnp.zeros((CSUB, FACE, load_cases), values.dtype)
    lower_face = jnp.concatenate([zero_rim, values[:SUBS - CSUB, FACE:2 * FACE]], axis=0)
    upper_face = jnp.concatenate([values[CSUB:, :FACE], zero_rim], axis=0)
    return jnp.concatenate([lower_face, upper_face, picked], axis=1)


def slot_weights(partner):
    cluster_of = jnp.arange(SUBS) // CSUB
    ones_face = jnp.ones((SUBS, FACE), jnp.float32)
    lower_face = jnp.where(cluster_of > 0, 0.5, 1.0).astype(jnp.float32)[:, None] * ones_face
    upper_face = jnp.where(cluster_of < CLUSTERS - 1, 0.5, 1.0).astype(jnp.float32)[:, None] * ones_face
    inner_rows = jnp.repeat(jnp.where(partner >= 0, 0.5, 1.0).astype(jnp.float32), BLK, axis=1)
    weight = jnp.concatenate([lower_face, upper_face, inner_rows], axis=1)
    return weight[:, :, None]


def precondition(vector, weight, basis_cluster, basis_global, cluster_inverse, global_inverse):
    load_cases = vector.shape[2]
    weighted = (weight * vector)[:, 2 * FACE:]
    cluster_terms = jnp.einsum("skn,snr->skr", basis_cluster, weighted, precision=PRECISE)
    global_terms = jnp.einsum("skn,snr->skr", basis_global, weighted, precision=PRECISE)
    cluster_sum = cluster_terms.reshape(CLUSTERS, CSUB, KC, load_cases).sum(axis=1)
    global_sum = global_terms.reshape(CLUSTERS, CSUB, MODES, load_cases).sum(axis=1)
    cluster_amounts = jnp.einsum("ckj,cjr->ckr", cluster_inverse, cluster_sum, precision=PRECISE)
    global_amounts = jnp.dot(global_inverse, global_sum.reshape(KG, load_cases), precision=PRECISE)
    global_amounts = global_amounts.reshape(CLUSTERS, MODES, load_cases)
    extra = jnp.einsum("skn,skr->snr", basis_cluster, jnp.repeat(cluster_amounts, CSUB, axis=0), precision=PRECISE)
    extra = extra + jnp.einsum("skn,skr->snr", basis_global, jnp.repeat(global_amounts, CSUB, axis=0), precision=PRECISE)
    return jnp.concatenate([vector[:, :2 * FACE], vector[:, 2 * FACE:] + extra], axis=1)


def reference(dual_ops, dual_rhs, partner, cluster_basis, global_basis, cluster_inverse, global_inverse):
    weight = slot_weights(partner)
    basis_cluster = cluster_basis.astype(jnp.float32)
    basis_global = global_basis.astype(jnp.float32)

    def apply_coarse(vector):
        return precondition(vector, weight, basis_cluster, basis_global, cluster_inverse, global_inverse)

    def inner_product(first, second):
        return jnp.sum(weight * first * second, axis=(0, 1))

    def subdomain_product(pair):
        return jnp.dot(pair[0], pair[1].astype(jnp.bfloat16), preferred_element_type=jnp.float32)

    def operate(direction):
        products = lax.map(subdomain_product, (dual_ops, direction))
        return products + partner_copy(products, partner)

    residual = dual_rhs.astype(jnp.float32)
    precond = apply_coarse(residual)
    direction = precond
    energy_now = inner_product(residual, precond)
    multipliers = jnp.zeros_like(residual)
    for iteration in range(ITERS):
        applied = operate(direction)
        step_size = energy_now / inner_product(direction, applied)
        multipliers = multipliers + step_size * direction
        residual = residual - step_size * applied
        precond = apply_coarse(residual)
        energy_next = inner_product(residual, precond)
        direction = precond + (energy_next / energy_now) * direction
        energy_now = energy_next
    return multipliers
```

```python
import jax
import jax.numpy as jnp
from jax import lax
from jax.experimental import pallas as pl
from jax.experimental.pallas import tpu as pltpu
from jax.sharding import PartitionSpec as P

FACE = 64
BLK = 32
MODES = 6
NIB = 28
RIM = 2 * FACE
CHUNK = 4
EXTRA = 16
GAMMA, DELTA, CROSS, CROSS_T = 6, 7, 8, 9

PRECISE = lax.Precision.HIGHEST
F32 = jnp.float32
BF16 = jnp.bfloat16


def split(value, parts):
    pieces = []
    for _ in range(parts):
        piece = value.astype(BF16)
        pieces.append(piece)
        value = value - piece.astype(F32)
    return pieces


def narrow_dot(narrow, value, parts, transposed=False):
    dims = (((0,), (0,)), ((), ())) if transposed else (((1,), (0,)), ((), ()))
    total = None
    for piece in reversed(split(value, parts)):
        term = lax.dot_general(narrow, piece, dims, preferred_element_type=F32)
        total = term if total is None else total + term
    return total


def wide_dot(first, second):
    return jnp.dot(first, second, precision=PRECISE, preferred_element_type=F32)


def column_sum(value):
    return jnp.sum(value, axis=0, keepdims=True)


def slot_row(index):
    return CHUNK * index + CHUNK - 1


def partner_rows(ids, incoming, block):
    target = ids[block]
    rows = incoming[jnp.maximum(target, 0)]
    return jnp.where(jnp.full(rows.shape, target, jnp.int32) >= 0, rows, 0.0)


def send_products(ids, products, out_blocks, low, high):
    low[...] = products[:FACE]
    high[...] = products[FACE:RIM]
    for block in range(NIB):
        target = ids[block]
        start = RIM + block * BLK

        @pl.when(target >= 0)
        def _():
            out_blocks[target] = products[start : start + BLK]


def set_row(ref, index, value):
    row = slot_row(index)
    ref[row : row + 1, :] = value


def one_hot(shape, test):
    rows = lax.broadcasted_iota(jnp.int32, shape, 0)
    columns = lax.broadcasted_iota(jnp.int32, shape, 1)
    return jnp.where(test(rows, columns), 1.0, 0.0)


def prepare_kernel(ids, rhs, cluster_basis, global_basis, inverse, global_inverse,
                   sums, basis, weight, solve, global_solve):
    cluster, last = ids[NIB], ids[NIB + 1]
    kc = cluster_basis.shape[0]
    rows = basis.shape[0]
    kg = global_inverse.shape[0]
    spread = one_hot((rows, kc), lambda i, j: i == j + j // (CHUNK - 1))
    spread_global = one_hot((rows, MODES), lambda i, j: i == CHUNK * j + CHUNK - 1)
    placed = jnp.dot(spread.astype(BF16), cluster_basis[...], preferred_element_type=F32)
    placed = placed + jnp.dot(
        spread_global.astype(BF16), global_basis[...], preferred_element_type=F32
    )
    basis[...] = placed.astype(BF16)
    shape = (FACE, weight.shape[1])
    weight[:FACE, :] = jnp.where(jnp.full(shape, cluster, jnp.int32) > 0, 0.5, 1.0)
    weight[FACE:RIM, :] = jnp.where(jnp.full(shape, cluster, jnp.int32) < last, 0.5, 1.0)
    for block in range(NIB):
        start = RIM + block * BLK
        weight[start : start + BLK, :] = jnp.where(
            jnp.full((BLK, weight.shape[1]), ids[block], jnp.int32) >= 0, 0.5, 1.0
        )
    weighted = weight[RIM:, :] * rhs[RIM:, :].astype(F32)
    sums[...] = narrow_dot(basis[...], weighted, 3)
    spread_t = one_hot((kc, rows), lambda i, j: j == i + i // (CHUNK - 1))
    solve[...] = wide_dot(wide_dot(spread, inverse[...]), spread_t)
    pick = one_hot(
        (rows, kg), lambda i, j: (i == CHUNK * (j - cluster * MODES) + CHUNK - 1)
        & (j >= cluster * MODES) & (j < (cluster + 1) * MODES)
    )
    place = one_hot(
        (kg, global_solve.shape[1]),
        lambda i, j: (j // EXTRA == i // MODES) & (j % EXTRA == i % MODES),
    )
    global_solve[...] = wide_dot(wide_dot(pick, global_inverse[...]), place)


def chunk_sum_kernel(parts, copies):
    rows, lanes = parts.shape
    tile = 2 * CHUNK
    total = jnp.sum(parts[...].reshape(rows // tile, tile, lanes), axis=0)
    total = total + pltpu.roll(total, CHUNK, 0)
    copies[...] = jnp.broadcast_to(total[None], (copies.shape[0] // tile, tile, lanes)).reshape(
        copies.shape
    )


def amounts(solve, global_solve, projection, global_projection):
    return wide_dot(solve[...], projection) + wide_dot(global_solve[...], global_projection)


def totals(gathered):
    rows, lanes = gathered.shape
    return jnp.sum(gathered[...].reshape(rows // EXTRA, EXTRA, lanes), axis=0)


def start_kernel(ids, rhs, operator, basis, weight, solve, global_solve, projection, gathered,
                 precond, products, sums, out_blocks, low, high):
    coarse = amounts(solve, global_solve, projection[...], gathered[...])
    extra = narrow_dot(basis[...], coarse, 3, transposed=True)
    precond[:RIM, :] = rhs[:RIM, :].astype(F32)
    precond[RIM:, :] = rhs[RIM:, :].astype(F32) + extra
    direction = precond[...]
    products[...] = narrow_dot(operator[...], direction, 1)
    send_products(ids, products, out_blocks, low, high)
    sums[...] = narrow_dot(basis[...], products[RIM:, :], 3)
    set_row(sums, GAMMA, column_sum(weight[...] * rhs[...].astype(F32) * direction))
    set_row(sums, DELTA, column_sum(direction * products[...]))


def store_applied(ids, applied, products, incoming, from_low, from_high):
    applied[:FACE, :] = products[:FACE, :] + from_low[...]
    applied[FACE:RIM, :] = products[FACE:RIM, :] + from_high[...]
    for block in range(NIB):
        start = RIM + block * BLK
        applied[start : start + BLK, :] = products[start : start + BLK, :] + partner_rows(
            ids, incoming, block
        )


def first_step_kernel(ids, rhs, operator, basis, weight, solve, global_solve,
                      projection, gathered, precond, products,
                      incoming, from_low, from_high, projection_a, gathered_a,
                      residual, applied, projection_new, gathered_new, scalars,
                      precond_new, products_new, sums, out_blocks, low, high):
    total = totals(gathered_a)
    gamma, curve = total[GAMMA : GAMMA + 1], total[DELTA : DELTA + 1]
    alpha = gamma / curve
    scalars[0:1, :] = gamma
    scalars[1:2, :] = curve
    scalars[2:3, :] = alpha
    projection_new[...] = projection[...] - alpha * projection_a[...]
    gathered_new[...] = gathered[...] - alpha * gathered_a[...]
    coarse = amounts(solve, global_solve, projection_new[...], gathered_new[...])
    extra = narrow_dot(basis[...], coarse, 3, transposed=True)
    store_applied(ids, applied, products, incoming, from_low, from_high)
    residual[...] = rhs[...].astype(F32) - alpha * applied[...]
    precond_new[:RIM, :] = residual[:RIM, :]
    precond_new[RIM:, :] = residual[RIM:, :] + extra
    products_new[...] = narrow_dot(operator[...], precond_new[...], 2)
    send_products(ids, products_new, out_blocks, low, high)
    sums[...] = narrow_dot(basis[...], products_new[RIM:, :], 3)
    set_row(sums, GAMMA, column_sum(weight[...] * residual[...] * precond_new[...]))
    set_row(sums, DELTA, column_sum(precond_new[...] * products_new[...]))
    set_row(sums, CROSS, column_sum(precond_new[...] * products[...]))
    set_row(sums, CROSS_T, column_sum(precond[...] * products_new[...]))


def conjugate(total, gamma_old, curve_old):
    gamma = total[GAMMA : GAMMA + 1]
    beta = gamma / gamma_old
    cross = total[CROSS : CROSS + 1] + total[CROSS_T : CROSS_T + 1]
    curve = total[DELTA : DELTA + 1] + beta * cross + beta * beta * curve_old
    return gamma, beta, curve, gamma / curve


def second_step_kernel(ids, operator, basis, weight, solve, global_solve,
                       residual, applied, projection, gathered, scalars,
                       precond_old, products_old, projection_old, gathered_old,
                       precond, products, incoming, from_low, from_high,
                       projection_a, gathered_a,
                       multipliers, direction, precond_new, scalars_new, copies, work, conj):
    gamma_old, curve_old = scalars[0:1, :], scalars[1:2, :]
    gamma, beta, curve, alpha = conjugate(totals(gathered_a), gamma_old, curve_old)
    scalars_new[0:1, :] = gamma
    scalars_new[1:2, :] = curve
    projection_new = projection[...] - alpha * (projection_a[...] + beta * projection_old[...])
    gathered_new = gathered[...] - alpha * (gathered_a[...] + beta * gathered_old[...])
    coarse = amounts(solve, global_solve, projection_new, gathered_new)
    extra = narrow_dot(basis[...], coarse, 3, transposed=True)
    direction[...] = precond[...] + beta * precond_old[...]
    multipliers[...] = scalars[2:3, :] * precond_old[...] + alpha * direction[...]
    conj[...] = products[...] + beta * products_old[...]
    store_applied(ids, work, products, incoming, from_low, from_high)
    work[...] = residual[...] - alpha * (work[...] + beta * applied[...])
    precond_new[:RIM, :] = work[:RIM, :]
    precond_new[RIM:, :] = work[RIM:, :] + extra
    gamma_part = column_sum(weight[...] * work[...] * precond_new[...])
    work[...] = narrow_dot(operator[...], precond_new[...], 2)
    rows = jnp.concatenate(
        [
            gamma_part,
            column_sum(precond_new[...] * work[...]),
            column_sum(precond_new[...] * conj[...]),
            column_sum(direction[...] * work[...]),
        ],
        axis=0,
    )
    tile = jnp.concatenate([rows, rows], axis=0)
    copies[...] = jnp.broadcast_to(
        tile[None], (copies.shape[0] // tile.shape[0],) + tile.shape
    ).reshape(copies.shape)


def last_step_kernel(multipliers, direction, precond, scalars, gathered, out):
    rows, lanes = gathered.shape
    tile = 2 * CHUNK
    total = jnp.sum(gathered[...].reshape(rows // tile, tile, lanes), axis=0)
    gamma = total[0:1]
    beta = gamma / scalars[0:1, :]
    curve = total[1:2] + beta * (total[2:3] + total[3:4]) + beta * beta * scalars[1:2, :]
    alpha = gamma / curve
    out[...] = multipliers[...] + alpha * (precond[...] + beta * direction[...])


def call(kernel, outs, args, scratch=(), smem=True):
    specs = [pl.BlockSpec(memory_space=pltpu.VMEM)] * len(args)
    if smem:
        specs[0] = pl.BlockSpec(memory_space=pltpu.SMEM)
    return pl.pallas_call(
        kernel,
        out_shape=[jax.ShapeDtypeStruct(shape, dtype) for shape, dtype in outs],
        in_specs=specs,
        out_specs=[pl.BlockSpec(memory_space=pltpu.VMEM)] * len(outs),
        scratch_shapes=[pltpu.VMEM(shape, dtype) for shape, dtype in scratch],
    )(*args)


def exchange(values):
    return lax.all_to_all(values, "sub", split_axis=0, concat_axis=0, tiled=True)


def on_device(
    dual_ops, dual_rhs, partner, cluster_basis, global_basis, cluster_inverse, global_inverse
):
    subs, clusters = lax.axis_size("sub"), lax.axis_size("clus")
    rhs = dual_rhs[0]
    operator = dual_ops[0]
    rows, lanes = rhs.shape
    partner_ids = partner[0]
    targets = jnp.where(partner_ids >= 0, partner_ids // NIB, -1).astype(jnp.int32)
    place = jnp.stack([lax.axis_index("clus"), jnp.int32(clusters - 1)]).astype(jnp.int32)
    ids = jnp.concatenate([targets, place, jnp.zeros((2,), jnp.int32)])
    n = subs * CHUNK
    vector = ((rows, lanes), F32)
    sums_out = ((n, lanes), F32)
    gathered_out = ((clusters * EXTRA, lanes), F32)
    scalar_out = ((8, lanes), F32)
    face = ((FACE, lanes), F32)
    blocks = ((subs, BLK, lanes), F32)

    def reduce_all(sums):
        (copies,) = call(chunk_sum_kernel, [sums_out], [exchange(sums)], smem=False)
        projection = exchange(copies)
        extra = lax.slice(
            projection, (CHUNK - 1, 0), (slot_row(EXTRA - 1) + 1, lanes), (CHUNK, 1)
        )
        return projection, lax.all_gather(extra, "clus", axis=0, tiled=True)

    def swap(out_blocks, low, high):
        up = [(i, i + 1) for i in range(clusters - 1)]
        down = [(i + 1, i) for i in range(clusters - 1)]
        from_low = lax.ppermute(high, "clus", up)
        from_high = lax.ppermute(low, "clus", down)
        return exchange(out_blocks), from_low, from_high

    sums, basis, weight, solve, global_solve = call(
        prepare_kernel,
        [sums_out, ((n, cluster_basis.shape[2]), BF16), vector, ((n, n), F32),
         ((n, clusters * EXTRA), F32)],
        [ids, rhs, cluster_basis[0], global_basis[0], cluster_inverse[0], global_inverse],
    )
    fixed = [basis, weight, solve, global_solve]
    projection, gathered = reduce_all(sums)

    precond, products, sums, out_blocks, low, high = call(
        start_kernel,
        [vector, vector, sums_out, blocks, face, face],
        [ids, rhs, operator, *fixed, projection, gathered],
    )
    swapped = swap(out_blocks, low, high)
    projection_a, gathered_a = reduce_all(sums)

    (residual, applied, projection_1, gathered_1, scalars, precond_1, products_1, sums,
     out_blocks, low, high) = call(
        first_step_kernel,
        [vector, vector, sums_out, gathered_out, scalar_out, vector, vector, sums_out,
         blocks, face, face],
        [ids, rhs, operator, *fixed, projection, gathered, precond, products, *swapped,
         projection_a, gathered_a],
    )
    swapped = swap(out_blocks, low, high)
    projection_b, gathered_b = reduce_all(sums)

    multipliers, direction, precond_2, scalars_1, copies = call(
        second_step_kernel,
        [vector, vector, vector, scalar_out, sums_out],
        [ids, operator, *fixed, residual, applied, projection_1, gathered_1, scalars,
         precond, products, projection_a, gathered_a, precond_1, products_1, *swapped,
         projection_b, gathered_b],
        scratch=[vector, vector],
    )
    (total,) = call(chunk_sum_kernel, [((2 * CHUNK, lanes), F32)], [exchange(copies)], smem=False)
    gathered_c = lax.all_gather(total, "clus", axis=0, tiled=True)
    (result,) = call(
        last_step_kernel, [vector], [multipliers, direction, precond_2, scalars_1, gathered_c],
        smem=False,
    )
    return result[None]


def solution(mesh):
    return jax.shard_map(
        on_device,
        mesh=mesh,
        in_specs=(
            P(("clus", "sub"), None, None),
            P(("clus", "sub"), None, None),
            P(("clus", "sub"), None),
            P(("clus", "sub"), None, None),
            P(("clus", "sub"), None, None),
            P("clus", None, None),
            P(),
        ),
        out_specs=P(("clus", "sub"), None, None),
        check_vma=False,
    )
```

```python
import jax
import jax.numpy as jnp
from jax import lax
from jax.experimental import pallas as pl
from jax.experimental.pallas import tpu as pltpu
from jax.sharding import PartitionSpec as P

FACE = 64
BLK = 32
MODES = 6
NIB = 28
RIM = 2 * FACE
NEAR = 4
CHUNK = 4
EXTRA = 16
GAMMA, DELTA, CROSS, CROSS_T = 6, 7, 8, 9

PRECISE = lax.Precision.HIGHEST
F32 = jnp.float32
BF16 = jnp.bfloat16


def split(value, parts):
    pieces = []
    for _ in range(parts):
        piece = value.astype(BF16)
        pieces.append(piece)
        value = value - piece.astype(F32)
    return pieces


def narrow_dot(narrow, value, parts):
    lanes = value.shape[1]
    pieces = jnp.concatenate(split(value, parts), axis=1)
    product = jnp.dot(narrow, pieces, preferred_element_type=F32)
    total = product[:, (parts - 1) * lanes :]
    for part in reversed(range(parts - 1)):
        total = total + product[:, part * lanes : (part + 1) * lanes]
    return total


def wide_dot(first, second):
    return jnp.dot(first, second, precision=PRECISE, preferred_element_type=F32)


def column_sum(value):
    return jnp.sum(value, axis=0, keepdims=True)


def slot_row(index):
    return CHUNK * index + CHUNK - 1


def partner_rows(ids, incoming, block):
    target = ids[block]
    rows = incoming[jnp.maximum(target, 0)]
    return jnp.where(jnp.full(rows.shape, target, jnp.int32) >= 0, rows, 0.0)


def send_products(ids, products, out_blocks, low, high):
    low[...] = products[:FACE]
    high[...] = products[FACE:RIM]
    for block in range(NIB):
        target = ids[block]
        start = RIM + block * BLK

        @pl.when(target >= 0)
        def _():
            out_blocks[target] = products[start : start + BLK]


def set_row(ref, index, value):
    row = slot_row(index)
    ref[row : row + 1, :] = value


def one_hot(shape, test):
    rows = lax.broadcasted_iota(jnp.int32, shape, 0)
    columns = lax.broadcasted_iota(jnp.int32, shape, 1)
    return jnp.where(test(rows, columns), 1.0, 0.0)


def prepare_kernel(ids, rhs, cluster_basis, global_basis, inverse, global_inverse,
                   sums, basis, basis_t, weight, solve, global_solve):
    cluster, last = ids[NIB], ids[NIB + 1]
    kc = cluster_basis.shape[0]
    rows = basis.shape[0]
    kg = global_inverse.shape[0]
    spread = one_hot((rows, kc), lambda i, j: i == j + j // (CHUNK - 1))
    spread_global = one_hot((rows, MODES), lambda i, j: i == CHUNK * j + CHUNK - 1)
    placed = jnp.dot(spread.astype(BF16), cluster_basis[...], preferred_element_type=F32)
    placed = placed + jnp.dot(
        spread_global.astype(BF16), global_basis[...], preferred_element_type=F32
    )
    basis[...] = placed.astype(BF16)
    basis_t[...] = placed.T.astype(BF16)
    shape = (FACE, weight.shape[1])
    weight[:FACE, :] = jnp.where(jnp.full(shape, cluster, jnp.int32) > 0, 0.5, 1.0)
    weight[FACE:RIM, :] = jnp.where(jnp.full(shape, cluster, jnp.int32) < last, 0.5, 1.0)
    for block in range(NIB):
        start = RIM + block * BLK
        weight[start : start + BLK, :] = jnp.where(
            jnp.full((BLK, weight.shape[1]), ids[block], jnp.int32) >= 0, 0.5, 1.0
        )
    weighted = weight[RIM:, :] * rhs[RIM:, :].astype(F32)
    sums[...] = narrow_dot(basis[...], weighted, 3)
    spread_t = one_hot((kc, rows), lambda i, j: j == i + i // (CHUNK - 1))
    solve[...] = wide_dot(wide_dot(spread, inverse[...]), spread_t)
    pick = one_hot(
        (rows, kg), lambda i, j: (i == CHUNK * (j - cluster * MODES) + CHUNK - 1)
        & (j >= cluster * MODES) & (j < (cluster + 1) * MODES)
    )
    place = one_hot(
        (kg, global_solve.shape[1]),
        lambda i, j: (j // EXTRA == i // MODES) & (j % EXTRA == i % MODES),
    )
    global_solve[...] = wide_dot(wide_dot(pick, global_inverse[...]), place)


def chunk_sum_kernel(parts, copies):
    rows, lanes = parts.shape
    tile = 2 * CHUNK
    total = jnp.sum(parts[...].reshape(rows // tile, tile, lanes), axis=0)
    total = total + pltpu.roll(total, CHUNK, 0)
    if copies.shape[0] <= tile:
        copies[...] = total[: copies.shape[0]]
    else:
        copies[...] = jnp.broadcast_to(
            total[None], (copies.shape[0] // tile, tile, lanes)
        ).reshape(copies.shape)


def amounts(solve, global_solve, projection, global_projection):
    return wide_dot(solve[...], projection) + wide_dot(global_solve[...], global_projection)


def totals(gathered):
    rows, lanes = gathered.shape
    return jnp.sum(gathered[...].reshape(rows // EXTRA, EXTRA, lanes), axis=0)


def start_kernel(ids, rhs, operator, basis, basis_t, weight, solve, global_solve, projection, gathered,
                 precond, products, sums, out_blocks, low, high):
    coarse = amounts(solve, global_solve, projection[...], gathered[...])
    extra = narrow_dot(basis_t[...], coarse, 3)
    precond[:RIM, :] = rhs[:RIM, :].astype(F32)
    precond[RIM:, :] = rhs[RIM:, :].astype(F32) + extra
    direction = precond[...]
    products[...] = narrow_dot(operator[...], direction, 1)
    send_products(ids, products, out_blocks, low, high)
    sums[...] = narrow_dot(basis[...], products[RIM:, :], 3)
    set_row(sums, GAMMA, column_sum(weight[...] * rhs[...].astype(F32) * direction))
    set_row(sums, DELTA, column_sum(direction * products[...]))


def store_applied(ids, applied, products, incoming, from_low, from_high):
    applied[:FACE, :] = products[:FACE, :] + from_low[...]
    applied[FACE:RIM, :] = products[FACE:RIM, :] + from_high[...]
    for block in range(NIB):
        start = RIM + block * BLK
        applied[start : start + BLK, :] = products[start : start + BLK, :] + partner_rows(
            ids, incoming, block
        )


def first_step_kernel(ids, rhs, operator, basis, basis_t, weight, solve, global_solve,
                      projection, gathered, precond, products,
                      incoming, from_low, from_high, projection_a, gathered_a,
                      residual, applied, projection_new, gathered_new, scalars,
                      precond_new, products_new, sums, out_blocks, low, high):
    total = totals(gathered_a)
    gamma, curve = total[GAMMA : GAMMA + 1], total[DELTA : DELTA + 1]
    alpha = gamma / curve
    scalars[0:1, :] = gamma
    scalars[1:2, :] = curve
    scalars[2:3, :] = alpha
    projection_new[...] = projection[...] - alpha * projection_a[...]
    gathered_new[...] = gathered[...] - alpha * gathered_a[...]
    coarse = amounts(solve, global_solve, projection_new[...], gathered_new[...])
    extra = narrow_dot(basis_t[...], coarse, 3)
    store_applied(ids, applied, products, incoming, from_low, from_high)
    residual[...] = rhs[...].astype(F32) - alpha * applied[...]
    precond_new[:RIM, :] = residual[:RIM, :]
    precond_new[RIM:, :] = residual[RIM:, :] + extra
    products_new[...] = narrow_dot(operator[...], precond_new[...], 2)
    send_products(ids, products_new, out_blocks, low, high)
    sums[...] = narrow_dot(basis[...], products_new[RIM:, :], 3)
    set_row(sums, GAMMA, column_sum(weight[...] * residual[...] * precond_new[...]))
    set_row(sums, DELTA, column_sum(precond_new[...] * products_new[...]))
    set_row(sums, CROSS, column_sum(precond_new[...] * products[...]))
    set_row(sums, CROSS_T, column_sum(precond[...] * products_new[...]))


def conjugate(total, gamma_old, curve_old):
    gamma = total[GAMMA : GAMMA + 1]
    beta = gamma / gamma_old
    cross = total[CROSS : CROSS + 1] + total[CROSS_T : CROSS_T + 1]
    curve = total[DELTA : DELTA + 1] + beta * cross + beta * beta * curve_old
    return gamma, beta, curve, gamma / curve


def second_step_kernel(ids, operator, basis, basis_t, weight, solve, global_solve,
                       residual, applied, projection, gathered, scalars,
                       precond_old, products_old, projection_old, gathered_old,
                       precond, products, incoming, from_low, from_high,
                       projection_a, gathered_a,
                       multipliers, direction, precond_new, scalars_new, copies, work, conj):
    gamma_old, curve_old = scalars[0:1, :], scalars[1:2, :]
    gamma, beta, curve, alpha = conjugate(totals(gathered_a), gamma_old, curve_old)
    scalars_new[0:1, :] = gamma
    scalars_new[1:2, :] = curve
    projection_new = projection[...] - alpha * (projection_a[...] + beta * projection_old[...])
    gathered_new = gathered[...] - alpha * (gathered_a[...] + beta * gathered_old[...])
    coarse = amounts(solve, global_solve, projection_new, gathered_new)
    extra = narrow_dot(basis_t[...], coarse, 3)
    direction[...] = precond[...] + beta * precond_old[...]
    multipliers[...] = scalars[2:3, :] * precond_old[...] + alpha * direction[...]
    conj[...] = products[...] + beta * products_old[...]
    store_applied(ids, work, products, incoming, from_low, from_high)
    work[...] = residual[...] - alpha * (work[...] + beta * applied[...])
    precond_new[:RIM, :] = work[:RIM, :]
    precond_new[RIM:, :] = work[RIM:, :] + extra
    gamma_part = column_sum(weight[...] * work[...] * precond_new[...])
    work[...] = narrow_dot(operator[...], precond_new[...], 2)
    rows = jnp.concatenate(
        [
            gamma_part,
            column_sum(precond_new[...] * work[...]),
            column_sum(precond_new[...] * conj[...]),
            column_sum(direction[...] * work[...]),
        ],
        axis=0,
    )
    tile = jnp.concatenate([rows, rows], axis=0)
    copies[...] = jnp.broadcast_to(
        tile[None], (copies.shape[0] // tile.shape[0],) + tile.shape
    ).reshape(copies.shape)


def last_step_kernel(multipliers, direction, precond, scalars, gathered, out):
    rows, lanes = gathered.shape
    tile = 2 * CHUNK
    total = jnp.sum(gathered[...].reshape(rows // tile, tile, lanes), axis=0)
    gamma = total[0:1]
    beta = gamma / scalars[0:1, :]
    curve = total[1:2] + beta * (total[2:3] + total[3:4]) + beta * beta * scalars[1:2, :]
    alpha = gamma / curve
    out[...] = multipliers[...] + alpha * (precond[...] + beta * direction[...])


def call(kernel, outs, args, scratch=(), smem=True):
    specs = [pl.BlockSpec(memory_space=pltpu.VMEM)] * len(args)
    if smem:
        specs[0] = pl.BlockSpec(memory_space=pltpu.SMEM)
    return pl.pallas_call(
        kernel,
        out_shape=[jax.ShapeDtypeStruct(shape, dtype) for shape, dtype in outs],
        in_specs=specs,
        out_specs=[pl.BlockSpec(memory_space=pltpu.VMEM)] * len(outs),
        scratch_shapes=[pltpu.VMEM(shape, dtype) for shape, dtype in scratch],
    )(*args)


def gather_subs(values):
    subs = lax.axis_size("sub")
    rows_of = [[far * NEAR + near for near in range(NEAR)] for far in range(subs // NEAR)]
    columns_of = [[far * NEAR + near for far in range(subs // NEAR)] for near in range(NEAR)]
    for groups in (rows_of, columns_of):
        values = lax.all_gather(values, "sub", axis=0, tiled=True, axis_index_groups=groups)
    return values


def exchange(values):
    return lax.all_to_all(values, "sub", split_axis=0, concat_axis=0, tiled=True)


def on_device(
    dual_ops, dual_rhs, partner, cluster_basis, global_basis, cluster_inverse, global_inverse
):
    subs, clusters = lax.axis_size("sub"), lax.axis_size("clus")
    rhs = dual_rhs[0]
    operator = dual_ops[0]
    rows, lanes = rhs.shape
    partner_ids = partner[0]
    targets = jnp.where(partner_ids >= 0, partner_ids // NIB, -1).astype(jnp.int32)
    place = jnp.stack([lax.axis_index("clus"), jnp.int32(clusters - 1)]).astype(jnp.int32)
    ids = jnp.concatenate([targets, place, jnp.zeros((2,), jnp.int32)])
    n = subs * CHUNK
    vector = ((rows, lanes), F32)
    sums_out = ((n, lanes), F32)
    gathered_out = ((clusters * EXTRA, lanes), F32)
    scalar_out = ((8, lanes), F32)
    face = ((FACE, lanes), F32)
    blocks = ((subs, BLK, lanes), F32)

    def reduce_all(sums, beside):
        shape = sums_out if not beside else ((CHUNK, lanes), F32)
        (copies,) = call(chunk_sum_kernel, [shape], [exchange(sums)], smem=False)
        projection = gather_subs(copies) if beside else exchange(copies)
        extra = lax.slice(
            projection, (CHUNK - 1, 0), (slot_row(EXTRA - 1) + 1, lanes), (CHUNK, 1)
        )
        return projection, lax.all_gather(extra, "clus", axis=0, tiled=True)

    def swap(out_blocks, low, high):
        up = [(i, i + 1) for i in range(clusters - 1)]
        down = [(i + 1, i) for i in range(clusters - 1)]
        from_low = lax.ppermute(high, "clus", up)
        from_high = lax.ppermute(low, "clus", down)
        return exchange(out_blocks), from_low, from_high

    sums, basis, basis_t, weight, solve, global_solve = call(
        prepare_kernel,
        [sums_out, ((n, cluster_basis.shape[2]), BF16), ((cluster_basis.shape[2], n), BF16), vector, ((n, n), F32),
         ((n, clusters * EXTRA), F32)],
        [ids, rhs, cluster_basis[0], global_basis[0], cluster_inverse[0], global_inverse],
    )
    fixed = [basis, basis_t, weight, solve, global_solve]
    projection, gathered = reduce_all(sums, False)

    precond, products, sums, out_blocks, low, high = call(
        start_kernel,
        [vector, vector, sums_out, blocks, face, face],
        [ids, rhs, operator, *fixed, projection, gathered],
    )
    swapped = swap(out_blocks, low, high)
    projection_a, gathered_a = reduce_all(sums, True)

    (residual, applied, projection_1, gathered_1, scalars, precond_1, products_1, sums,
     out_blocks, low, high) = call(
        first_step_kernel,
        [vector, vector, sums_out, gathered_out, scalar_out, vector, vector, sums_out,
         blocks, face, face],
        [ids, rhs, operator, *fixed, projection, gathered, precond, products, *swapped,
         projection_a, gathered_a],
    )
    swapped = swap(out_blocks, low, high)
    projection_b, gathered_b = reduce_all(sums, True)

    multipliers, direction, precond_2, scalars_1, copies = call(
        second_step_kernel,
        [vector, vector, vector, scalar_out, sums_out],
        [ids, operator, *fixed, residual, applied, projection_1, gathered_1, scalars,
         precond, products, projection_a, gathered_a, precond_1, products_1, *swapped,
         projection_b, gathered_b],
        scratch=[vector, vector],
    )
    (total,) = call(chunk_sum_kernel, [((2 * CHUNK, lanes), F32)], [exchange(copies)], smem=False)
    gathered_c = lax.all_gather(total, "clus", axis=0, tiled=True)
    (result,) = call(
        last_step_kernel, [vector], [multipliers, direction, precond_2, scalars_1, gathered_c],
        smem=False,
    )
    return result[None]


def solution(mesh):
    return jax.shard_map(
        on_device,
        mesh=mesh,
        in_specs=(
            P(("clus", "sub"), None, None),
            P(("clus", "sub"), None, None),
            P(("clus", "sub"), None),
            P(("clus", "sub"), None, None),
            P(("clus", "sub"), None, None),
            P("clus", None, None),
            P(),
        ),
        out_specs=P(("clus", "sub"), None, None),
        check_vma=False,
    )
```

```python
import jax
import jax.numpy as jnp
from jax import lax
from jax.experimental import pallas as pl
from jax.experimental.pallas import tpu as pltpu
from jax.sharding import PartitionSpec as P

FACE = 64
BLK = 32
MODES = 6
NIB = 28
RIM = 2 * FACE
NEAR = 4
CHUNK = 4
EXTRA = 16
GAMMA, DELTA, CROSS, CROSS_T = 6, 7, 8, 9

PRECISE = lax.Precision.HIGHEST
F32 = jnp.float32
BF16 = jnp.bfloat16


def split(value, parts):
    pieces = []
    for _ in range(parts):
        piece = value.astype(BF16)
        pieces.append(piece)
        value = value - piece.astype(F32)
    return pieces


def narrow_dot(narrow, value, parts):
    lanes = value.shape[1]
    pieces = jnp.concatenate(split(value, parts), axis=1)
    product = jnp.dot(narrow, pieces, preferred_element_type=F32)
    total = product[:, (parts - 1) * lanes :]
    for part in reversed(range(parts - 1)):
        total = total + product[:, part * lanes : (part + 1) * lanes]
    return total


def wide_dot(first, second):
    return jnp.dot(first, second, precision=PRECISE, preferred_element_type=F32)


def column_sum(value):
    return jnp.sum(value, axis=0, keepdims=True)


def slot_row(index):
    return CHUNK * index + CHUNK - 1


def partner_rows(ids, incoming, block):
    target = ids[block]
    rows = incoming[jnp.maximum(target, 0)]
    return jnp.where(jnp.full(rows.shape, target, jnp.int32) >= 0, rows, 0.0)


def send_products(ids, products, out_blocks, low, high):
    low[...] = products[:FACE]
    high[...] = products[FACE:RIM]
    for block in range(NIB):
        target = ids[block]
        start = RIM + block * BLK

        @pl.when(target >= 0)
        def _():
            out_blocks[target] = products[start : start + BLK]


def set_row(ref, index, value):
    row = slot_row(index)
    ref[row : row + 1, :] = value


def one_hot(shape, test):
    rows = lax.broadcasted_iota(jnp.int32, shape, 0)
    columns = lax.broadcasted_iota(jnp.int32, shape, 1)
    return jnp.where(test(rows, columns), 1.0, 0.0)


def prepare_kernel(ids, rhs, cluster_basis, global_basis, inverse, global_inverse,
                   sums, basis, basis_t, weight, solve, global_solve):
    cluster, last = ids[NIB], ids[NIB + 1]
    kc = cluster_basis.shape[0]
    rows = basis.shape[0]
    kg = global_inverse.shape[0]
    spread = one_hot((rows, kc), lambda i, j: i == j + j // (CHUNK - 1))
    spread_global = one_hot((rows, MODES), lambda i, j: i == CHUNK * j + CHUNK - 1)
    placed = jnp.dot(spread.astype(BF16), cluster_basis[...], preferred_element_type=F32)
    placed = placed + jnp.dot(
        spread_global.astype(BF16), global_basis[...], preferred_element_type=F32
    )
    basis[...] = placed.astype(BF16)
    basis_t[...] = placed.T.astype(BF16)
    shape = (FACE, weight.shape[1])
    weight[:FACE, :] = jnp.where(jnp.full(shape, cluster, jnp.int32) > 0, 0.5, 1.0)
    weight[FACE:RIM, :] = jnp.where(jnp.full(shape, cluster, jnp.int32) < last, 0.5, 1.0)
    for block in range(NIB):
        start = RIM + block * BLK
        weight[start : start + BLK, :] = jnp.where(
            jnp.full((BLK, weight.shape[1]), ids[block], jnp.int32) >= 0, 0.5, 1.0
        )
    weighted = weight[RIM:, :] * rhs[RIM:, :].astype(F32)
    sums[...] = narrow_dot(basis[...], weighted, 3)
    spread_t = one_hot((kc, rows), lambda i, j: j == i + i // (CHUNK - 1))
    solve[...] = wide_dot(wide_dot(spread, inverse[...]), spread_t)
    pick = one_hot(
        (rows, kg), lambda i, j: (i == CHUNK * (j - cluster * MODES) + CHUNK - 1)
        & (j >= cluster * MODES) & (j < (cluster + 1) * MODES)
    )
    place = one_hot(
        (kg, global_solve.shape[1]),
        lambda i, j: (j // EXTRA == i // MODES) & (j % EXTRA == i % MODES),
    )
    global_solve[...] = wide_dot(wide_dot(pick, global_inverse[...]), place)


def chunk_sum_kernel(parts, copies):
    rows, lanes = parts.shape
    tile = 2 * CHUNK
    total = jnp.sum(parts[...].reshape(rows // tile, tile, lanes), axis=0)
    total = total + pltpu.roll(total, CHUNK, 0)
    if copies.shape[0] <= tile:
        copies[...] = total[: copies.shape[0]]
    else:
        copies[...] = jnp.broadcast_to(
            total[None], (copies.shape[0] // tile, tile, lanes)
        ).reshape(copies.shape)


def far_sum_kernel(parts, copies):
    rows, lanes = parts.shape
    far = lax.axis_size("sub") // NEAR
    total = jnp.sum(parts[...].reshape(far, rows // far, lanes), axis=0)
    copies[...] = jnp.broadcast_to(total[None], (far,) + total.shape).reshape(rows, lanes)


def near_sum_kernel(parts, total, extra):
    rows, lanes = total.shape
    total[...] = jnp.sum(parts[...].reshape(NEAR, rows, lanes), axis=0)
    for index in range(EXTRA):
        row = slot_row(index)
        extra[index : index + 1, :] = total[row : row + 1, :]


def amounts(solve, global_solve, projection, global_projection):
    return wide_dot(solve[...], projection) + wide_dot(global_solve[...], global_projection)


def totals(gathered):
    rows, lanes = gathered.shape
    return jnp.sum(gathered[...].reshape(rows // EXTRA, EXTRA, lanes), axis=0)


def start_kernel(ids, rhs, operator, basis, basis_t, weight, solve, global_solve, projection, gathered,
                 precond, products, sums, out_blocks, low, high):
    coarse = amounts(solve, global_solve, projection[...], gathered[...])
    extra = narrow_dot(basis_t[...], coarse, 3)
    precond[:RIM, :] = rhs[:RIM, :].astype(F32)
    precond[RIM:, :] = rhs[RIM:, :].astype(F32) + extra
    direction = precond[...]
    products[...] = narrow_dot(operator[...], direction, 1)
    send_products(ids, products, out_blocks, low, high)
    sums[...] = narrow_dot(basis[...], products[RIM:, :], 3)
    set_row(sums, GAMMA, column_sum(weight[...] * rhs[...].astype(F32) * direction))
    set_row(sums, DELTA, column_sum(direction * products[...]))


def store_applied(ids, applied, products, incoming, from_low, from_high):
    applied[:FACE, :] = products[:FACE, :] + from_low[...]
    applied[FACE:RIM, :] = products[FACE:RIM, :] + from_high[...]
    for block in range(NIB):
        start = RIM + block * BLK
        applied[start : start + BLK, :] = products[start : start + BLK, :] + partner_rows(
            ids, incoming, block
        )


def first_step_kernel(ids, rhs, operator, basis, basis_t, weight, solve, global_solve,
                      projection, gathered, precond, products,
                      incoming, from_low, from_high, projection_a, gathered_a,
                      residual, applied, projection_new, gathered_new, scalars,
                      precond_new, products_new, sums, out_blocks, low, high):
    total = totals(gathered_a)
    gamma, curve = total[GAMMA : GAMMA + 1], total[DELTA : DELTA + 1]
    alpha = gamma / curve
    scalars[0:1, :] = gamma
    scalars[1:2, :] = curve
    scalars[2:3, :] = alpha
    projection_new[...] = projection[...] - alpha * projection_a[...]
    gathered_new[...] = gathered[...] - alpha * gathered_a[...]
    coarse = amounts(solve, global_solve, projection_new[...], gathered_new[...])
    extra = narrow_dot(basis_t[...], coarse, 3)
    store_applied(ids, applied, products, incoming, from_low, from_high)
    residual[...] = rhs[...].astype(F32) - alpha * applied[...]
    precond_new[:RIM, :] = residual[:RIM, :]
    precond_new[RIM:, :] = residual[RIM:, :] + extra
    products_new[...] = narrow_dot(operator[...], precond_new[...], 2)
    send_products(ids, products_new, out_blocks, low, high)
    sums[...] = narrow_dot(basis[...], products_new[RIM:, :], 3)
    set_row(sums, GAMMA, column_sum(weight[...] * residual[...] * precond_new[...]))
    set_row(sums, DELTA, column_sum(precond_new[...] * products_new[...]))
    set_row(sums, CROSS, column_sum(precond_new[...] * products[...]))
    set_row(sums, CROSS_T, column_sum(precond[...] * products_new[...]))


def conjugate(total, gamma_old, curve_old):
    gamma = total[GAMMA : GAMMA + 1]
    beta = gamma / gamma_old
    cross = total[CROSS : CROSS + 1] + total[CROSS_T : CROSS_T + 1]
    curve = total[DELTA : DELTA + 1] + beta * cross + beta * beta * curve_old
    return gamma, beta, curve, gamma / curve


def second_step_kernel(ids, operator, basis, basis_t, weight, solve, global_solve,
                       residual, applied, projection, gathered, scalars,
                       precond_old, products_old, projection_old, gathered_old,
                       precond, products, incoming, from_low, from_high,
                       projection_a, gathered_a,
                       multipliers, direction, precond_new, scalars_new, copies, work, conj):
    gamma_old, curve_old = scalars[0:1, :], scalars[1:2, :]
    gamma, beta, curve, alpha = conjugate(totals(gathered_a), gamma_old, curve_old)
    scalars_new[0:1, :] = gamma
    scalars_new[1:2, :] = curve
    projection_new = projection[...] - alpha * (projection_a[...] + beta * projection_old[...])
    gathered_new = gathered[...] - alpha * (gathered_a[...] + beta * gathered_old[...])
    coarse = amounts(solve, global_solve, projection_new, gathered_new)
    extra = narrow_dot(basis_t[...], coarse, 3)
    direction[...] = precond[...] + beta * precond_old[...]
    multipliers[...] = scalars[2:3, :] * precond_old[...] + alpha * direction[...]
    conj[...] = products[...] + beta * products_old[...]
    store_applied(ids, work, products, incoming, from_low, from_high)
    work[...] = residual[...] - alpha * (work[...] + beta * applied[...])
    precond_new[:RIM, :] = work[:RIM, :]
    precond_new[RIM:, :] = work[RIM:, :] + extra
    gamma_part = column_sum(weight[...] * work[...] * precond_new[...])
    work[...] = narrow_dot(operator[...], precond_new[...], 2)
    rows = jnp.concatenate(
        [
            gamma_part,
            column_sum(precond_new[...] * work[...]),
            column_sum(precond_new[...] * conj[...]),
            column_sum(direction[...] * work[...]),
        ],
        axis=0,
    )
    tile = jnp.concatenate([rows, rows], axis=0)
    copies[...] = jnp.broadcast_to(
        tile[None], (copies.shape[0] // tile.shape[0],) + tile.shape
    ).reshape(copies.shape)


def last_step_kernel(multipliers, direction, precond, scalars, gathered, out):
    rows, lanes = gathered.shape
    tile = 2 * CHUNK
    total = jnp.sum(gathered[...].reshape(rows // tile, tile, lanes), axis=0)
    gamma = total[0:1]
    beta = gamma / scalars[0:1, :]
    curve = total[1:2] + beta * (total[2:3] + total[3:4]) + beta * beta * scalars[1:2, :]
    alpha = gamma / curve
    out[...] = multipliers[...] + alpha * (precond[...] + beta * direction[...])


def call(kernel, outs, args, scratch=(), smem=True):
    specs = [pl.BlockSpec(memory_space=pltpu.VMEM)] * len(args)
    if smem:
        specs[0] = pl.BlockSpec(memory_space=pltpu.SMEM)
    return pl.pallas_call(
        kernel,
        out_shape=[jax.ShapeDtypeStruct(shape, dtype) for shape, dtype in outs],
        in_specs=specs,
        out_specs=[pl.BlockSpec(memory_space=pltpu.VMEM)] * len(outs),
        scratch_shapes=[pltpu.VMEM(shape, dtype) for shape, dtype in scratch],
    )(*args)


def near_groups():
    subs = lax.axis_size("sub")
    return [[far * NEAR + near for near in range(NEAR)] for far in range(subs // NEAR)]


def far_groups():
    subs = lax.axis_size("sub")
    return [[far * NEAR + near for far in range(subs // NEAR)] for near in range(NEAR)]


def exchange_far(values):
    return lax.all_to_all(
        values, "sub", split_axis=0, concat_axis=0, tiled=True, axis_index_groups=far_groups()
    )


def exchange(values):
    return lax.all_to_all(values, "sub", split_axis=0, concat_axis=0, tiled=True)


def on_device(
    dual_ops, dual_rhs, partner, cluster_basis, global_basis, cluster_inverse, global_inverse
):
    subs, clusters = lax.axis_size("sub"), lax.axis_size("clus")
    rhs = dual_rhs[0]
    operator = dual_ops[0]
    rows, lanes = rhs.shape
    partner_ids = partner[0]
    targets = jnp.where(partner_ids >= 0, partner_ids // NIB, -1).astype(jnp.int32)
    place = jnp.stack([lax.axis_index("clus"), jnp.int32(clusters - 1)]).astype(jnp.int32)
    ids = jnp.concatenate([targets, place, jnp.zeros((2,), jnp.int32)])
    n = subs * CHUNK
    vector = ((rows, lanes), F32)
    sums_out = ((n, lanes), F32)
    gathered_out = ((clusters * EXTRA, lanes), F32)
    scalar_out = ((8, lanes), F32)
    face = ((FACE, lanes), F32)
    blocks = ((subs, BLK, lanes), F32)

    def reduce_first(sums):
        (copies,) = call(chunk_sum_kernel, [sums_out], [exchange(sums)], smem=False)
        projection = exchange(copies)
        extra = lax.slice(
            projection, (CHUNK - 1, 0), (slot_row(EXTRA - 1) + 1, lanes), (CHUNK, 1)
        )
        return projection, lax.all_gather(extra, "clus", axis=0, tiled=True)

    def reduce_beside(sums):
        (copies,) = call(far_sum_kernel, [sums_out], [exchange_far(sums)], smem=False)
        column = exchange_far(copies)
        parts = lax.all_gather(
            column, "sub", axis=0, tiled=True, axis_index_groups=near_groups()
        )
        projection, extra = call(
            near_sum_kernel, [sums_out, ((EXTRA, lanes), F32)], [parts], smem=False
        )
        return projection, lax.all_gather(extra, "clus", axis=0, tiled=True)

    def swap(out_blocks, low, high):
        up = [(i, i + 1) for i in range(clusters - 1)]
        down = [(i + 1, i) for i in range(clusters - 1)]
        from_low = lax.ppermute(high, "clus", up)
        from_high = lax.ppermute(low, "clus", down)
        return exchange(out_blocks), from_low, from_high

    sums, basis, basis_t, weight, solve, global_solve = call(
        prepare_kernel,
        [sums_out, ((n, cluster_basis.shape[2]), BF16), ((cluster_basis.shape[2], n), BF16), vector, ((n, n), F32),
         ((n, clusters * EXTRA), F32)],
        [ids, rhs, cluster_basis[0], global_basis[0], cluster_inverse[0], global_inverse],
    )
    fixed = [basis, basis_t, weight, solve, global_solve]
    projection, gathered = reduce_first(sums)

    precond, products, sums, out_blocks, low, high = call(
        start_kernel,
        [vector, vector, sums_out, blocks, face, face],
        [ids, rhs, operator, *fixed, projection, gathered],
    )
    swapped = swap(out_blocks, low, high)
    projection_a, gathered_a = reduce_beside(sums)

    (residual, applied, projection_1, gathered_1, scalars, precond_1, products_1, sums,
     out_blocks, low, high) = call(
        first_step_kernel,
        [vector, vector, sums_out, gathered_out, scalar_out, vector, vector, sums_out,
         blocks, face, face],
        [ids, rhs, operator, *fixed, projection, gathered, precond, products, *swapped,
         projection_a, gathered_a],
    )
    swapped = swap(out_blocks, low, high)
    projection_b, gathered_b = reduce_beside(sums)

    multipliers, direction, precond_2, scalars_1, copies = call(
        second_step_kernel,
        [vector, vector, vector, scalar_out, sums_out],
        [ids, operator, *fixed, residual, applied, projection_1, gathered_1, scalars,
         precond, products, projection_a, gathered_a, precond_1, products_1, *swapped,
         projection_b, gathered_b],
        scratch=[vector, vector],
    )
    (total,) = call(chunk_sum_kernel, [((2 * CHUNK, lanes), F32)], [exchange(copies)], smem=False)
    gathered_c = lax.all_gather(total, "clus", axis=0, tiled=True)
    (result,) = call(
        last_step_kernel, [vector], [multipliers, direction, precond_2, scalars_1, gathered_c],
        smem=False,
    )
    return result[None]


def solution(mesh):
    return jax.shard_map(
        on_device,
        mesh=mesh,
        in_specs=(
            P(("clus", "sub"), None, None),
            P(("clus", "sub"), None, None),
            P(("clus", "sub"), None),
            P(("clus", "sub"), None, None),
            P(("clus", "sub"), None, None),
            P("clus", None, None),
            P(),
        ),
        out_specs=P(("clus", "sub"), None, None),
        check_vma=False,
    )
```

```python
import jax
import jax.numpy as jnp
from jax import lax
from jax.experimental import pallas as pl
from jax.experimental.pallas import tpu as pltpu
from jax.sharding import PartitionSpec as P

FACE = 64
BLK = 32
MODES = 6
NIB = 28
RIM = 2 * FACE
NEAR = 4
CHUNK = 4
EXTRA = 16
GAMMA, DELTA, CROSS, CROSS_T = 6, 7, 8, 9

PRECISE = lax.Precision.HIGHEST
F32 = jnp.float32
BF16 = jnp.bfloat16


def split(value, parts):
    pieces = []
    for _ in range(parts):
        piece = value.astype(BF16)
        pieces.append(piece)
        value = value - piece.astype(F32)
    return pieces


def narrow_dot(narrow, value, parts):
    lanes = value.shape[1]
    pieces = jnp.concatenate(split(value, parts), axis=1)
    product = jnp.dot(narrow, pieces, preferred_element_type=F32)
    total = product[:, (parts - 1) * lanes :]
    for part in reversed(range(parts - 1)):
        total = total + product[:, part * lanes : (part + 1) * lanes]
    return total


def wide_dot(first, second):
    return jnp.dot(first, second, precision=PRECISE, preferred_element_type=F32)


def column_sum(value):
    return jnp.sum(value, axis=0, keepdims=True)


def slot_row(index):
    return CHUNK * index + CHUNK - 1


def partner_rows(ids, incoming, block):
    target = ids[block]
    rows = incoming[jnp.maximum(target, 0)]
    return jnp.where(jnp.full(rows.shape, target, jnp.int32) >= 0, rows, 0.0)


def send_products(ids, products, out_blocks, low, high):
    low[...] = products[:FACE]
    high[...] = products[FACE:RIM]
    for block in range(NIB):
        target = ids[block]
        start = RIM + block * BLK

        @pl.when(target >= 0)
        def _():
            out_blocks[target] = products[start : start + BLK]


def set_row(ref, index, value):
    row = slot_row(index)
    ref[row : row + 1, :] = value


def one_hot(shape, test):
    rows = lax.broadcasted_iota(jnp.int32, shape, 0)
    columns = lax.broadcasted_iota(jnp.int32, shape, 1)
    return jnp.where(test(rows, columns), 1.0, 0.0)


def prepare_kernel(ids, rhs, cluster_basis, global_basis, inverse, global_inverse,
                   sums, basis, basis_t, weight, solve, global_solve):
    cluster, last = ids[NIB], ids[NIB + 1]
    kc = cluster_basis.shape[0]
    rows = basis.shape[0]
    kg = global_inverse.shape[0]
    spread = one_hot((rows, kc), lambda i, j: i == j + j // (CHUNK - 1))
    spread_global = one_hot((rows, MODES), lambda i, j: i == CHUNK * j + CHUNK - 1)
    placed = jnp.dot(spread.astype(BF16), cluster_basis[...], preferred_element_type=F32)
    placed = placed + jnp.dot(
        spread_global.astype(BF16), global_basis[...], preferred_element_type=F32
    )
    basis[...] = placed.astype(BF16)
    basis_t[...] = placed.T.astype(BF16)
    shape = (FACE, weight.shape[1])
    weight[:FACE, :] = jnp.where(jnp.full(shape, cluster, jnp.int32) > 0, 0.5, 1.0)
    weight[FACE:RIM, :] = jnp.where(jnp.full(shape, cluster, jnp.int32) < last, 0.5, 1.0)
    for block in range(NIB):
        start = RIM + block * BLK
        weight[start : start + BLK, :] = jnp.where(
            jnp.full((BLK, weight.shape[1]), ids[block], jnp.int32) >= 0, 0.5, 1.0
        )
    weighted = weight[RIM:, :] * rhs[RIM:, :].astype(F32)
    total = narrow_dot(basis[...], weighted, 3)
    rigid = narrow_dot(global_basis[...], weighted, 3)
    pad = jnp.zeros((2 * CHUNK - MODES, rigid.shape[1]), F32)
    rigid = jnp.concatenate([rigid, pad], axis=0)
    tiles = total.reshape(sums.shape[0], 2 * CHUNK, sums.shape[2])
    turned = pltpu.roll(rigid, CHUNK, 0)[None]
    first = lax.broadcasted_iota(jnp.int32, tiles.shape, 1) < CHUNK
    sums[:, : 2 * CHUNK, :] = jnp.where(first, tiles, turned)
    sums[:, 2 * CHUNK : 4 * CHUNK, :] = jnp.where(first, turned, tiles)
    sums[:, 4 * CHUNK :, :] = jnp.broadcast_to(rigid[None], tiles.shape)
    spread_t = one_hot((kc, rows), lambda i, j: j == i + i // (CHUNK - 1))
    solve[...] = wide_dot(wide_dot(spread, inverse[...]), spread_t)
    pick = one_hot(
        (rows, kg), lambda i, j: (i == CHUNK * (j - cluster * MODES) + CHUNK - 1)
        & (j >= cluster * MODES) & (j < (cluster + 1) * MODES)
    )
    place = one_hot(
        (kg, global_solve.shape[1]),
        lambda i, j: (j // EXTRA == i // MODES) & (j % EXTRA == i % MODES),
    )
    global_solve[...] = wide_dot(wide_dot(pick, global_inverse[...]), place)


def chunk_sum_kernel(parts, copies):
    rows, lanes = parts.shape
    tile = 2 * CHUNK
    total = jnp.sum(parts[...].reshape(rows // tile, tile, lanes), axis=0)
    total = total + pltpu.roll(total, CHUNK, 0)
    if copies.shape[0] <= tile:
        copies[...] = total[: copies.shape[0]]
    else:
        copies[...] = jnp.broadcast_to(
            total[None], (copies.shape[0] // tile, tile, lanes)
        ).reshape(copies.shape)


def first_sum_kernel(parts, copies, extra):
    rows, lanes = copies.shape
    tile = 2 * CHUNK
    total = jnp.sum(parts[...], axis=0)
    even, odd, rigid = total[:tile], total[tile : 2 * tile], total[2 * tile :]
    first = lax.broadcasted_iota(jnp.int32, even.shape, 0) < CHUNK
    chunk = jnp.where(first, even, odd)
    chunk = chunk + pltpu.roll(chunk, CHUNK, 0)
    copies[...] = jnp.broadcast_to(chunk[None], (rows // tile, tile, lanes)).reshape(rows, lanes)
    extra[:tile, :] = rigid + pltpu.roll(jnp.where(first, odd, even), CHUNK, 0)
    extra[tile:, :] = jnp.zeros((EXTRA - tile, lanes), F32)


def far_sum_kernel(parts, copies):
    rows, lanes = parts.shape
    far = lax.axis_size("sub") // NEAR
    total = jnp.sum(parts[...].reshape(far, rows // far, lanes), axis=0)
    copies[...] = jnp.broadcast_to(total[None], (far,) + total.shape).reshape(rows, lanes)


def near_sum_kernel(parts, total, extra):
    rows, lanes = total.shape
    total[...] = jnp.sum(parts[...].reshape(NEAR, rows, lanes), axis=0)
    for index in range(EXTRA):
        row = slot_row(index)
        extra[index : index + 1, :] = total[row : row + 1, :]


def amounts(solve, global_solve, projection, global_projection):
    return wide_dot(solve[...], projection) + wide_dot(global_solve[...], global_projection)


def totals(gathered):
    rows, lanes = gathered.shape
    return jnp.sum(gathered[...].reshape(rows // EXTRA, EXTRA, lanes), axis=0)


def start_kernel(ids, rhs, operator, basis, basis_t, weight, solve, global_solve, projection, gathered,
                 precond, products, sums, out_blocks, low, high):
    coarse = amounts(solve, global_solve, projection[...], gathered[...])
    extra = narrow_dot(basis_t[...], coarse, 3)
    precond[:RIM, :] = rhs[:RIM, :].astype(F32)
    precond[RIM:, :] = rhs[RIM:, :].astype(F32) + extra
    direction = precond[...]
    products[...] = narrow_dot(operator[...], direction, 1)
    send_products(ids, products, out_blocks, low, high)
    sums[...] = narrow_dot(basis[...], products[RIM:, :], 3)
    set_row(sums, GAMMA, column_sum(weight[...] * rhs[...].astype(F32) * direction))
    set_row(sums, DELTA, column_sum(direction * products[...]))


def store_applied(ids, applied, products, incoming, from_low, from_high):
    applied[:FACE, :] = products[:FACE, :] + from_low[...]
    applied[FACE:RIM, :] = products[FACE:RIM, :] + from_high[...]
    for block in range(NIB):
        start = RIM + block * BLK
        applied[start : start + BLK, :] = products[start : start + BLK, :] + partner_rows(
            ids, incoming, block
        )


def first_step_kernel(ids, rhs, operator, basis, basis_t, weight, solve, global_solve,
                      projection, gathered, precond, products,
                      incoming, from_low, from_high, projection_a, gathered_a,
                      residual, applied, projection_new, gathered_new, scalars,
                      precond_new, products_new, sums, out_blocks, low, high):
    total = totals(gathered_a)
    gamma, curve = total[GAMMA : GAMMA + 1], total[DELTA : DELTA + 1]
    alpha = gamma / curve
    scalars[0:1, :] = gamma
    scalars[1:2, :] = curve
    scalars[2:3, :] = alpha
    projection_new[...] = projection[...] - alpha * projection_a[...]
    gathered_new[...] = gathered[...] - alpha * gathered_a[...]
    coarse = amounts(solve, global_solve, projection_new[...], gathered_new[...])
    extra = narrow_dot(basis_t[...], coarse, 3)
    store_applied(ids, applied, products, incoming, from_low, from_high)
    residual[...] = rhs[...].astype(F32) - alpha * applied[...]
    precond_new[:RIM, :] = residual[:RIM, :]
    precond_new[RIM:, :] = residual[RIM:, :] + extra
    products_new[...] = narrow_dot(operator[...], precond_new[...], 2)
    send_products(ids, products_new, out_blocks, low, high)
    sums[...] = narrow_dot(basis[...], products_new[RIM:, :], 3)
    set_row(sums, GAMMA, column_sum(weight[...] * residual[...] * precond_new[...]))
    set_row(sums, DELTA, column_sum(precond_new[...] * products_new[...]))
    set_row(sums, CROSS, column_sum(precond_new[...] * products[...]))
    set_row(sums, CROSS_T, column_sum(precond[...] * products_new[...]))


def conjugate(total, gamma_old, curve_old):
    gamma = total[GAMMA : GAMMA + 1]
    beta = gamma / gamma_old
    cross = total[CROSS : CROSS + 1] + total[CROSS_T : CROSS_T + 1]
    curve = total[DELTA : DELTA + 1] + beta * cross + beta * beta * curve_old
    return gamma, beta, curve, gamma / curve


def second_step_kernel(ids, operator, basis, basis_t, weight, solve, global_solve,
                       residual, applied, projection, gathered, scalars,
                       precond_old, products_old, projection_old, gathered_old,
                       precond, products, incoming, from_low, from_high,
                       projection_a, gathered_a,
                       multipliers, direction, precond_new, scalars_new, copies, work, conj):
    gamma_old, curve_old = scalars[0:1, :], scalars[1:2, :]
    gamma, beta, curve, alpha = conjugate(totals(gathered_a), gamma_old, curve_old)
    scalars_new[0:1, :] = gamma
    scalars_new[1:2, :] = curve
    projection_new = projection[...] - alpha * (projection_a[...] + beta * projection_old[...])
    gathered_new = gathered[...] - alpha * (gathered_a[...] + beta * gathered_old[...])
    coarse = amounts(solve, global_solve, projection_new, gathered_new)
    extra = narrow_dot(basis_t[...], coarse, 3)
    direction[...] = precond[...] + beta * precond_old[...]
    multipliers[...] = scalars[2:3, :] * precond_old[...] + alpha * direction[...]
    conj[...] = products[...] + beta * products_old[...]
    store_applied(ids, work, products, incoming, from_low, from_high)
    work[...] = residual[...] - alpha * (work[...] + beta * applied[...])
    precond_new[:RIM, :] = work[:RIM, :]
    precond_new[RIM:, :] = work[RIM:, :] + extra
    gamma_part = column_sum(weight[...] * work[...] * precond_new[...])
    work[...] = narrow_dot(operator[...], precond_new[...], 2)
    rows = jnp.concatenate(
        [
            gamma_part,
            column_sum(precond_new[...] * work[...]),
            column_sum(precond_new[...] * conj[...]),
            column_sum(direction[...] * work[...]),
        ],
        axis=0,
    )
    tile = jnp.concatenate([rows, rows], axis=0)
    copies[...] = jnp.broadcast_to(
        tile[None], (copies.shape[0] // tile.shape[0],) + tile.shape
    ).reshape(copies.shape)


def last_step_kernel(multipliers, direction, precond, scalars, gathered, out):
    rows, lanes = gathered.shape
    tile = 2 * CHUNK
    total = jnp.sum(gathered[...].reshape(rows // tile, tile, lanes), axis=0)
    gamma = total[0:1]
    beta = gamma / scalars[0:1, :]
    curve = total[1:2] + beta * (total[2:3] + total[3:4]) + beta * beta * scalars[1:2, :]
    alpha = gamma / curve
    out[...] = multipliers[...] + alpha * (precond[...] + beta * direction[...])


def call(kernel, outs, args, scratch=(), smem=True):
    specs = [pl.BlockSpec(memory_space=pltpu.VMEM)] * len(args)
    if smem:
        specs[0] = pl.BlockSpec(memory_space=pltpu.SMEM)
    return pl.pallas_call(
        kernel,
        out_shape=[jax.ShapeDtypeStruct(shape, dtype) for shape, dtype in outs],
        in_specs=specs,
        out_specs=[pl.BlockSpec(memory_space=pltpu.VMEM)] * len(outs),
        scratch_shapes=[pltpu.VMEM(shape, dtype) for shape, dtype in scratch],
    )(*args)


def near_groups():
    subs = lax.axis_size("sub")
    return [[far * NEAR + near for near in range(NEAR)] for far in range(subs // NEAR)]


def far_groups():
    subs = lax.axis_size("sub")
    return [[far * NEAR + near for far in range(subs // NEAR)] for near in range(NEAR)]


def exchange_far(values):
    return lax.all_to_all(
        values, "sub", split_axis=0, concat_axis=0, tiled=True, axis_index_groups=far_groups()
    )


def exchange(values):
    return lax.all_to_all(values, "sub", split_axis=0, concat_axis=0, tiled=True)


def on_device(
    dual_ops, dual_rhs, partner, cluster_basis, global_basis, cluster_inverse, global_inverse
):
    subs, clusters = lax.axis_size("sub"), lax.axis_size("clus")
    rhs = dual_rhs[0]
    operator = dual_ops[0]
    rows, lanes = rhs.shape
    partner_ids = partner[0]
    targets = jnp.where(partner_ids >= 0, partner_ids // NIB, -1).astype(jnp.int32)
    place = jnp.stack([lax.axis_index("clus"), jnp.int32(clusters - 1)]).astype(jnp.int32)
    ids = jnp.concatenate([targets, place, jnp.zeros((2,), jnp.int32)])
    n = subs * CHUNK
    vector = ((rows, lanes), F32)
    sums_out = ((n, lanes), F32)
    gathered_out = ((clusters * EXTRA, lanes), F32)
    scalar_out = ((8, lanes), F32)
    face = ((FACE, lanes), F32)
    blocks = ((subs, BLK, lanes), F32)

    def reduce_first(sums):
        parts = exchange(sums.reshape(3 * subs, CHUNK, lanes)).reshape(sums.shape)
        copies, extra = call(
            first_sum_kernel, [sums_out, ((EXTRA, lanes), F32)], [parts], smem=False
        )
        return exchange(copies), lax.all_gather(extra, "clus", axis=0, tiled=True)

    def reduce_beside(sums):
        (copies,) = call(far_sum_kernel, [sums_out], [exchange_far(sums)], smem=False)
        column = exchange_far(copies)
        parts = lax.all_gather(
            column, "sub", axis=0, tiled=True, axis_index_groups=near_groups()
        )
        projection, extra = call(
            near_sum_kernel, [sums_out, ((EXTRA, lanes), F32)], [parts], smem=False
        )
        return projection, lax.all_gather(extra, "clus", axis=0, tiled=True)

    def swap(out_blocks, low, high):
        up = [(i, i + 1) for i in range(clusters - 1)]
        down = [(i + 1, i) for i in range(clusters - 1)]
        from_low = lax.ppermute(high, "clus", up)
        from_high = lax.ppermute(low, "clus", down)
        return exchange(out_blocks), from_low, from_high

    sums, basis, basis_t, weight, solve, global_solve = call(
        prepare_kernel,
        [((subs // 2, 6 * CHUNK, lanes), F32), ((n, cluster_basis.shape[2]), BF16), ((cluster_basis.shape[2], n), BF16), vector, ((n, n), F32),
         ((n, clusters * EXTRA), F32)],
        [ids, rhs, cluster_basis[0], global_basis[0], cluster_inverse[0], global_inverse],
    )
    fixed = [basis, basis_t, weight, solve, global_solve]
    projection, gathered = reduce_first(sums)

    precond, products, sums, out_blocks, low, high = call(
        start_kernel,
        [vector, vector, sums_out, blocks, face, face],
        [ids, rhs, operator, *fixed, projection, gathered],
    )
    swapped = swap(out_blocks, low, high)
    projection_a, gathered_a = reduce_beside(sums)

    (residual, applied, projection_1, gathered_1, scalars, precond_1, products_1, sums,
     out_blocks, low, high) = call(
        first_step_kernel,
        [vector, vector, sums_out, gathered_out, scalar_out, vector, vector, sums_out,
         blocks, face, face],
        [ids, rhs, operator, *fixed, projection, gathered, precond, products, *swapped,
         projection_a, gathered_a],
    )
    swapped = swap(out_blocks, low, high)
    projection_b, gathered_b = reduce_beside(sums)

    multipliers, direction, precond_2, scalars_1, copies = call(
        second_step_kernel,
        [vector, vector, vector, scalar_out, sums_out],
        [ids, operator, *fixed, residual, applied, projection_1, gathered_1, scalars,
         precond, products, projection_a, gathered_a, precond_1, products_1, *swapped,
         projection_b, gathered_b],
        scratch=[vector, vector],
    )
    (total,) = call(chunk_sum_kernel, [((2 * CHUNK, lanes), F32)], [exchange(copies)], smem=False)
    gathered_c = lax.all_gather(total, "clus", axis=0, tiled=True)
    (result,) = call(
        last_step_kernel, [vector], [multipliers, direction, precond_2, scalars_1, gathered_c],
        smem=False,
    )
    return result[None]


def solution(mesh):
    return jax.shard_map(
        on_device,
        mesh=mesh,
        in_specs=(
            P(("clus", "sub"), None, None),
            P(("clus", "sub"), None, None),
            P(("clus", "sub"), None),
            P(("clus", "sub"), None, None),
            P(("clus", "sub"), None, None),
            P("clus", None, None),
            P(),
        ),
        out_specs=P(("clus", "sub"), None, None),
        check_vma=False,
    )
```
